32 devices in a mesh: groups: 2 (over y), wide: 4 (over z), narrow: 2 (over x), inner: 2 (over core).
Axes of the slice: x: 2, y: 2, z: 4, core: 2. Of those that a mesh axis runs over, the one named last changes fastest.
Arguments:
- tokens: bfloat16 [128, 6144], P(('groups', 'wide'), ('narrow', 'inner')), parts along dimension 0, may hold values from -6 to 6
- cotangent: bfloat16 [128, 6144], P(('groups', 'wide'), ('narrow', 'inner')), parts along dimension 0, may hold values from -3 to 3
- w_gate: bfloat16 [6144, 16384], P(('narrow', 'inner'), 'wide'), may hold values from -0.078125 to 0.078125
- w_up: bfloat16 [6144, 16384], P(('narrow', 'inner'), 'wide'), may hold values from -0.078125 to 0.078125
- w_down: bfloat16 [16384, 6144], P('wide', ('narrow', 'inner')), may hold values from -0.046875 to 0.046875
Outputs:
- output: bfloat16 [128, 6144], P(('groups', 'wide'), ('narrow', 'inner')), parts along dimension 0
- grad_input: bfloat16 [128, 6144], P(('groups', 'wide'), ('narrow', 'inner')), parts along dimension 0
- grad_wgate: bfloat16 [12288, 16384], P(('groups', 'narrow', 'inner'), 'wide'), parts along dimension 0
- grad_wup: bfloat16 [12288, 16384], P(('groups', 'narrow', 'inner'), 'wide'), parts along dimension 0
- grad_wdown: bfloat16 [32768, 6144], P(('groups', 'wide'), ('narrow', 'inner')), parts along dimension 0
The draws below stay inside these ranges and needn't reach their ends.
There are 2 independent parts, one for each index of `groups`. The reference program is written for one: setup_inputs(seed, part) draws one part's arguments, and reference() takes and returns one part's arrays. A program takes and returns all parts, laid end to end along the dimension named above; an argument that names none is the same for every part. Nothing has to cross between parts.
All inputs are finite; a program needn't handle non-finite values.
Results may differ from the reference program's by a relative error of at most 0.012.
Values may be sent and summed in bfloat16 or wider, within the bound.
No kernel may reach another device: no remote copies, remote signals or barrier semaphores. Data moves between devices by JAX's collectives and lax.ppermute only.
A program may use at most 192 MiB of HBM per device.

```python
import jax
import jax.numpy as jnp
from jax import lax

D = 6144
FF = 16384
TOKENS = 64


def block_scale(key, extent, cuts, smallest, top_value):
    level = 1.0
    for dim, shards_of in cuts:
        heights = jax.random.uniform(jax.random.fold_in(jax.random.fold_in(key, 6), dim), (shards_of,), jnp.float32, smallest / len(cuts), top_value / len(cuts))
        level = level * jnp.repeat(jnp.exp(heights), extent[dim] // shards_of).reshape((-1,) + (1,) * (len(extent) - 1 - dim))
    return level


def noise(own_key, extent, scale, most, pieces=(), held_as=jnp.bfloat16):
    entries = scale * jax.random.normal(own_key, extent, jnp.float32)
    if pieces:
        entries = entries * block_scale(own_key, extent, pieces, -0.22, 0.18)
    return jnp.clip(entries, -most, most).astype(held_as)


def setup_inputs(seed: int = 0, part: int = 0) -> dict:
    keys = jax.random.split(jax.random.key(seed), 6)
    part_splits = jax.random.split(jax.random.fold_in(keys[5], part), 6)
    tokens = noise(part_splits[0], (TOKENS, D), 1.0, 6.0, ((0, 4), (1, 4)))
    cotangent = noise(part_splits[1], (TOKENS, D), 0.5, 3.0, ((0, 4), (1, 4)))
    w_gate = noise(keys[2], (D, FF), D ** -0.5, 0.078125, ((0, 4), (1, 4)))
    w_up = noise(keys[3], (D, FF), D ** -0.5, 0.078125, ((0, 4), (1, 4)))
    w_down = noise(keys[4], (FF, D), FF ** -0.5, 0.046875, ((0, 4), (1, 4)))
    return dict(tokens=tokens, cotangent=cotangent, w_gate=w_gate, w_up=w_up, w_down=w_down)


def contract_last(left, right):
    return lax.dot_general(left, right, (((1,), (1,)), ((), ())), preferred_element_type=jnp.float32)


def contract_first(left, right):
    return lax.dot_general(left, right, (((0,), (0,)), ((), ())), preferred_element_type=jnp.float32)


def reference(tokens, cotangent, w_gate, w_up, w_down):
    gate = jnp.dot(tokens, w_gate, preferred_element_type=jnp.float32)
    up = jnp.dot(tokens, w_up, preferred_element_type=jnp.float32)
    sigmoid_gate = jax.nn.sigmoid(gate)
    hidden = (gate * sigmoid_gate * up).astype(jnp.bfloat16)
    output = jnp.dot(hidden, w_down, preferred_element_type=jnp.float32).astype(jnp.bfloat16)
    upstream = contract_last(cotangent, w_down)
    grad_wdown = contract_first(hidden, cotangent).astype(jnp.bfloat16)
    grad_gate = (upstream * up * sigmoid_gate * (1.0 + gate * (1.0 - sigmoid_gate))).astype(jnp.bfloat16)
    grad_up = (upstream * gate * sigmoid_gate).astype(jnp.bfloat16)
    grad_input = (contract_last(grad_gate, w_gate) + contract_last(grad_up, w_up)).astype(jnp.bfloat16)
    grad_wgate = contract_first(tokens, grad_gate).astype(jnp.bfloat16)
    grad_wup = contract_first(tokens, grad_up).astype(jnp.bfloat16)
    return (output, grad_input, grad_wgate, grad_wup, grad_wdown)
```

```python
import functools

import jax
import jax.numpy as jnp
from jax import lax
from jax.experimental import pallas as pl
from jax.experimental.pallas import tpu as pltpu
from jax.sharding import PartitionSpec as P

F32 = jnp.float32
BF16 = jnp.bfloat16
CHUNKS = 2
VMEM_SPEC = pl.BlockSpec(memory_space=pltpu.VMEM)
SMEM_SPEC = pl.BlockSpec(memory_space=pltpu.SMEM)
HBM_SPEC = pl.BlockSpec(memory_space=pltpu.MemorySpace.HBM)
LIMIT = 6 << 20
SCALE = 100


def contract(left, right, left_dim, right_dim):
    return lax.dot_general(
        left, right, (((left_dim,), (right_dim,)), ((), ())), preferred_element_type=F32
    )


def params(**more):
    return pltpu.CompilerParams(vmem_limit_bytes=LIMIT, **more)


def cost(flops, moved):
    return pl.CostEstimate(
        flops=int(flops) // SCALE, bytes_accessed=int(moved) // SCALE, transcendentals=0
    )


def shift(x, axis, size, by):
    return lax.ppermute(x, axis, [(i, (i + by) % size) for i in range(size)])


def column(me_ref, part, inner, width):
    chunk, core = part
    return pl.multiple_of((chunk * inner + lax.rem(me_ref[0] + core, inner)) * width, 128)


def in_vmem(shape, dtype):
    return pltpu.VMEM(shape, dtype)


def in_hbm(x):
    return pltpu.with_memory_space_constraint(x, pltpu.MemorySpace.HBM)


def part_copies(start, whole, part, sems):
    here = pl.ds(start, part[2].shape[0])
    return [
        pltpu.make_async_copy(whole[0].at[:, here], part[0], sems.at[0]),
        pltpu.make_async_copy(whole[1].at[:, here], part[1], sems.at[1]),
        pltpu.make_async_copy(whole[2].at[here, :], part[2], sems.at[2]),
    ]


def part_shapes(weights, width):
    features = weights[0].shape[0]
    return [
        in_vmem((features, width), BF16),
        in_vmem((features, width), BF16),
        in_vmem((width, features), BF16),
    ]


def load_kernel(parts, inner, *refs):
    me, whole, out, sems = refs[0], refs[1:4], refs[4:-1], refs[-1]
    copies = []
    for i, part in enumerate(parts):
        dest = out[3 * i : 3 * i + 3]
        start = column(me, part, inner, dest[2].shape[0])
        copies += part_copies(start, whole, dest, sems.at[i])
    for copy in copies:
        copy.start()
    for copy in copies:
        copy.wait()


def load(me, parts, inner, weights, width):
    outs = part_shapes(weights, width) * len(parts)
    out = pl.pallas_call(
        functools.partial(load_kernel, parts, inner),
        in_specs=[SMEM_SPEC] + [HBM_SPEC] * 3,
        out_specs=[VMEM_SPEC] * len(outs),
        out_shape=outs,
        scratch_shapes=[pltpu.SemaphoreType.DMA((len(parts), 3))],
        compiler_params=params(),
        cost_estimate=cost(0, 6 * len(parts) * width * weights[0].shape[0]),
        name="load_weights",
    )(me, *weights)
    return [tuple(out[3 * i : 3 * i + 3]) for i in range(len(parts))]


def pack_kernel(tokens, cot, packed):
    rows = tokens.shape[0]
    packed[:rows, :] = tokens[...]
    packed[rows:, :] = cot[...]


def pack(tokens, cot):
    return pl.pallas_call(
        pack_kernel,
        in_specs=[VMEM_SPEC] * 2,
        out_specs=VMEM_SPEC,
        out_shape=in_vmem((2 * tokens.shape[0], tokens.shape[1]), BF16),
        compiler_params=params(),
        name="pack_rows",
    )(tokens, cot)


def forward_kernel(rows, tile, pieces, loads, inner, out_dtype, *refs):
    refs = list(refs)
    take = lambda n: [refs.pop(0) for _ in range(n)]
    me = take(1)[0] if loads else None
    acts, weights = take(pieces or 2), take(3)
    whole = take(3) if loads else None
    sums = take(1)[0]
    if pieces:
        tokens_ref, cot_ref = take(2)
    else:
        tokens_ref, cot_ref = acts
    copies = []
    if loads:
        part = take(3)
        start = column(me, loads, inner, part[2].shape[0])
        copies = part_copies(start, whole, part, take(1)[0])
    for copy in copies:
        copy.start()
    if pieces:
        for k, piece in enumerate(acts):
            tokens_ref[pl.ds(k * rows, rows), :] = piece[:rows, :]
            cot_ref[pl.ds(k * rows, rows), :] = piece[rows:, :]

    def columns(step):
        here = pl.ds(pl.multiple_of(step * tile, 128), tile)
        tokens, cot = tokens_ref[...], cot_ref[...]
        sums[0, :, here] = contract(tokens, weights[0][:, here], 1, 0).astype(out_dtype)
        sums[1, :, here] = contract(tokens, weights[1][:, here], 1, 0).astype(out_dtype)
        sums[2, :, here] = contract(cot, weights[2][here, :], 1, 1).astype(out_dtype)

    steps = sums.shape[2] // tile
    if loads:
        pl.loop(0, steps)(columns)
    else:
        for step in range(steps):
            columns(step)
    for copy in copies:
        copy.wait()


def forward(me, inner, acts, part, rows, out_dtype, loads=(), whole=()):
    pieces = len(acts) if len(acts) != 2 else 0
    whole = whole if loads else ()
    width, features = part[2].shape
    total = rows * pieces if pieces else acts[0].shape[0]
    outs = [in_vmem((3, total, width), out_dtype)]
    if pieces:
        outs += [in_vmem((total, features), BF16)] * 2
    if loads:
        outs += part_shapes(whole, width)
    return pl.pallas_call(
        functools.partial(
            forward_kernel, rows, min(256, width), pieces, loads, inner, out_dtype
        ),
        in_specs=[SMEM_SPEC] * bool(loads)
        + [VMEM_SPEC] * (len(acts) + 3)
        + [HBM_SPEC] * len(whole),
        out_specs=[VMEM_SPEC] * len(outs),
        out_shape=outs,
        scratch_shapes=[pltpu.SemaphoreType.DMA((3,))] * bool(loads),
        compiler_params=params(),
        cost_estimate=cost(6 * total * width * features, 6 * width * features),
        name="partial_sums",
    )(*([me] * bool(loads)), *acts, *part, *whole)


def join_kernel(mine, received, kept, sent):
    total = mine[...] + received[...].astype(F32)
    kept[...] = total
    sent[...] = total.astype(BF16)


def join(mine, received):
    return pl.pallas_call(
        join_kernel,
        in_specs=[VMEM_SPEC] * 2,
        out_specs=[VMEM_SPEC] * 2,
        out_shape=[in_vmem(mine.shape, F32), in_vmem(mine.shape, BF16)],
        compiler_params=params(),
        cost_estimate=cost(mine.size, 12 * mine.size),
        name="join_cores",
    )(mine, received)


def activate_kernel(*refs):
    kept, received, out = refs[0], refs[1:-1], refs[-1]
    gate, up, upstream = [
        sum((r[i].astype(F32) for r in received), kept[i]) for i in range(3)
    ]
    sigmoid = 1.0 / (1.0 + jnp.exp(-gate))
    swish = gate * sigmoid
    out[0] = (swish * up).astype(BF16)
    out[1] = (upstream * up * sigmoid * (1.0 + gate * (1.0 - sigmoid))).astype(BF16)
    out[2] = (upstream * swish).astype(BF16)


def activate(kept, received):
    return pl.pallas_call(
        activate_kernel,
        in_specs=[VMEM_SPEC] * (1 + len(received)),
        out_specs=VMEM_SPEC,
        out_shape=in_vmem(kept.shape, BF16),
        compiler_params=params(),
        cost_estimate=cost(8 * kept.size, 8 * kept.size),
        name="activation",
    )(kept, *received)


def backward_kernel(where, inner, tile, rows, grads, first, fresh, last, *refs):
    refs = list(refs)
    take = lambda n: [refs.pop(0) for _ in range(n)]
    parts = len(where)
    me = take(1)[0]
    acts = take(parts)
    weights = [take(3) for _ in range(parts)] if rows else None
    tokens, cot = take(2) if grads else (None, None)
    before = take(2) if rows and not first else None
    if grads and not fresh:
        take(3)
    sums = take(1 + last if last else 2) if rows else None
    outs = take(3) if grads else None
    out_acc, grad_acc = (take(2) if last else sums) if rows else (None, None)
    if grads:
        wide, tall, sems = take(3)
    width = acts[0].shape[2]
    steps = width // tile

    def copies(slot, at):
        here = pl.ds(pl.multiple_of(at, 128), tile)
        return [
            pltpu.make_async_copy(wide.at[slot, 0], outs[0].at[:, here], sems.at[slot, 0]),
            pltpu.make_async_copy(wide.at[slot, 1], outs[1].at[:, here], sems.at[slot, 1]),
            pltpu.make_async_copy(tall.at[slot], outs[2].at[here, :], sems.at[slot, 2]),
        ]

    if rows:
        if first:
            out_acc[...] = jnp.zeros_like(out_acc)
            grad_acc[...] = jnp.zeros_like(grad_acc)
        else:
            out_acc[...] = before[0][...]
            grad_acc[...] = before[1][...]
    count = 0
    for p in range(parts):
        for j in range(steps):
            here = slice(j * tile, (j + 1) * tile)
            hidden, grad_gate, grad_up = [acts[p][i, :, here] for i in range(3)]
            if grads:
                slot = count % 2
                at = column(me, where[p], inner, width) + j * tile
                if count >= 2:
                    for copy in copies(slot, at):
                        copy.wait()
                wide[slot, 0] = contract(tokens[...], grad_gate, 0, 0).astype(BF16)
                wide[slot, 1] = contract(tokens[...], grad_up, 0, 0).astype(BF16)
                tall[slot] = contract(hidden, cot[...], 0, 0).astype(BF16)
                for copy in copies(slot, at):
                    copy.start()
            if rows:
                w_gate, w_up, w_down = weights[p]
                out_acc[...] += contract(hidden, w_down[here, :], 1, 0)
                grad_acc[...] += contract(grad_gate, w_gate[:, here], 1, 1) + contract(
                    grad_up, w_up[:, here], 1, 1
                )
            count += 1
    if last:
        n = sums[0].shape[0] // 2
        for k, ref in enumerate(sums):
            ref[:n, :] = out_acc[k * n : (k + 1) * n, :].astype(ref.dtype)
            ref[n:, :] = grad_acc[k * n : (k + 1) * n, :].astype(ref.dtype)
    if grads:
        for back in range(min(2, count)):
            for copy in copies((count - 1 - back) % 2, 0):
                copy.wait()


def backward(me, where, inner, acts, weights, tokens, cot, before, grads, hidden, last_rows=0):
    parts = len(acts)
    total, width = acts[0].shape[1:]
    features = tokens.shape[1]
    rows, makes = before is not None, grads is not None
    tile = min(256, width)
    args, specs, outs, out_specs, scratch = [me, *acts], [], [], [], []
    if rows:
        args += [w for part in weights for w in part]
    if makes:
        args += [tokens, cot]
    if rows:
        args += before
    specs = [SMEM_SPEC] + [VMEM_SPEC] * (len(args) - 1)
    aliases = {}
    if rows:
        if last_rows:
            shape = (2 * last_rows, features)
            outs += [in_vmem(shape, F32)] + [in_vmem(shape, BF16)] * (total // last_rows - 1)
            scratch += [pltpu.VMEM((total, features), F32)] * 2
        else:
            outs += [in_vmem((total, features), F32)] * 2
        out_specs += [VMEM_SPEC] * len(outs)
    if makes:
        aliases = {len(args) + i: len(outs) + i for i in range(len(grads))}
        args += grads
        specs += [HBM_SPEC] * len(grads)
        outs += [
            pltpu.HBM((features, hidden), BF16),
            pltpu.HBM((features, hidden), BF16),
            pltpu.HBM((hidden, features), BF16),
        ]
        out_specs += [HBM_SPEC] * 3
        scratch += [
            pltpu.VMEM((2, 2, features, tile), BF16),
            pltpu.VMEM((2, tile, features), BF16),
            pltpu.SemaphoreType.DMA((2, 3)),
        ]
    work = 6 * total * width * features * parts
    out = pl.pallas_call(
        functools.partial(
            backward_kernel, where, inner, tile, rows, makes, not before, not grads,
            total // last_rows - 1 if last_rows else 0,
        ),
        in_specs=specs,
        out_specs=out_specs,
        out_shape=outs,
        scratch_shapes=scratch,
        input_output_aliases=aliases,
        compiler_params=params(),
        cost_estimate=cost(work * (rows + makes), 6 * width * features * parts * (rows + makes)),
        name="output_rows" if not makes else "weight_grads" if not rows else "backward",
    )(*args)
    return (out[:-3], out[-3:]) if makes else (out, None)


def finish_kernel(*refs):
    mine, received, (output, grad_input) = refs[0], refs[1:-2], refs[-2:]
    rows = output.shape[0]
    total = mine[...]
    for r in received:
        total = total + r[...].astype(F32)
    output[...] = total[:rows].astype(BF16)
    grad_input[...] = total[rows:].astype(BF16)


def finish(mine, received):
    shape = jax.ShapeDtypeStruct((mine.shape[0] // 2, mine.shape[1]), BF16)
    return pl.pallas_call(
        finish_kernel,
        in_specs=[VMEM_SPEC] * (1 + len(received)),
        out_specs=[VMEM_SPEC] * 2,
        out_shape=[shape] * 2,
        compiler_params=params(),
        name="finish_rows",
    )(mine, *received)


def body(sizes, tokens, cotangent, w_gate, w_up, w_down):
    wide, narrow, inner = sizes["wide"], sizes["narrow"], sizes["inner"]
    rows = tokens.shape[0]
    hidden = w_gate.shape[1]
    weights = tuple(in_hbm(w) for w in (w_gate, w_up, w_down))
    width = hidden // (CHUNKS * inner)
    me = lax.axis_index("inner").astype(jnp.int32).reshape(1)
    order = [(c, core) for c in range(CHUNKS) for core in (1, 0)]

    packed = pack(tokens, cotangent)
    acts = [packed] + [shift(packed, "wide", wide, k) for k in range(1, wide)]
    parts = load(me, order[:2], inner, weights, width)
    acts, parts = lax.optimization_barrier((acts, parts))
    kept, sent, crossed = [], [], []
    for chunk in range(CHUNKS):
        at = 2 * chunk
        made = []
        for i, dtype in ((at, BF16), (at + 1, F32)):
            ahead = order[i + 2] if i + 2 < len(order) else ()
            out = forward(me, inner, acts, parts[i], rows, dtype, ahead, weights)
            made.append(out[0])
            if len(acts) != 2:
                acts = out[1:3]
            if ahead:
                parts.append(tuple(out[-3:]))
        total, out = join(made[1], shift(made[0], "inner", inner, 1))
        kept.append(total)
        sent.append(out)
        acts, _ = lax.optimization_barrier((acts, out))
        crossed.append([shift(out, "narrow", narrow, k) for k in range(1, narrow)])
    tokens_all, cot_all = acts
    crossed[0], _ = lax.optimization_barrier((crossed[0], sent))
    sums, grads, later = (), (), None
    for chunk in range(CHUNKS):
        at = 2 * chunk
        own = activate(kept[chunk], crossed[chunk])
        other = shift(own, "inner", inner, 1)
        both = [(order[at + 1], own, parts[at + 1]), (order[at], other, parts[at])]
        if chunk < CHUNKS - 1:
            where, what, which = zip(*both)
            sums, grads = backward(
                me, where, inner, what, which, tokens_all, cot_all, sums, grads, hidden
            )
            crossed[chunk + 1], sums = lax.optimization_barrier((crossed[chunk + 1], sums))
        else:
            for i, (where, what, which) in enumerate(both):
                sums, _ = backward(
                    me, [where], inner, [what], [which], tokens_all, cot_all, sums, None,
                    hidden, rows if i else 0,
                )
            where, what, _ = zip(*both)
    back = [shift(sums[k], "wide", wide, -k) for k in range(1, wide)]
    _, grads = backward(
        me, where, inner, what, None, tokens_all, cot_all, None, grads, hidden
    )
    output, grad_input = finish(sums[0], back)
    return (output, grad_input, *grads)


def solution(mesh):
    rows = P(("groups", "wide"), ("narrow", "inner"))
    return jax.shard_map(
        functools.partial(body, dict(mesh.shape)),
        mesh=mesh,
        in_specs=(
            rows,
            rows,
            P(("narrow", "inner"), "wide"),
            P(("narrow", "inner"), "wide"),
            P("wide", ("narrow", "inner")),
        ),
        out_specs=(
            rows,
            rows,
            P(("groups", "narrow", "inner"), "wide"),
            P(("groups", "narrow", "inner"), "wide"),
            P(("groups", "wide"), ("narrow", "inner")),
        ),
        check_vma=False,
    )
```

```python
import functools

import jax
import jax.numpy as jnp
from jax import lax
from jax.experimental import pallas as pl
from jax.experimental.pallas import tpu as pltpu
from jax.sharding import PartitionSpec as P

F32 = jnp.float32
BF16 = jnp.bfloat16
CHUNKS = ((4,), (4, 4), (4,))
VMEM_SPEC = pl.BlockSpec(memory_space=pltpu.VMEM)
SMEM_SPEC = pl.BlockSpec(memory_space=pltpu.SMEM)
ANY_SPEC = pl.BlockSpec(memory_space=pl.ANY)
HBM_SPEC = pl.BlockSpec(memory_space=pltpu.MemorySpace.HBM)
LIMIT = 10 << 20
SLOTS = 3


def contract(left, right, left_dim, right_dim):
    return lax.dot_general(
        left, right, (((left_dim,), (right_dim,)), ((), ())), preferred_element_type=F32
    )


def tile_of(width):
    return 256 if width % 256 == 0 else 128


def params(**more):
    return pltpu.CompilerParams(vmem_limit_bytes=LIMIT, **more)


def cost(flops, moved):
    return pl.CostEstimate(flops=int(flops), bytes_accessed=int(moved), transcendentals=0)


def shift(x, axis, size, by):
    return lax.ppermute(x, axis, [(i, (i + by) % size) for i in range(size)])


def column(me_ref, piece):
    start, core, inner, stride, at, _ = piece
    return pl.multiple_of(start + lax.rem(me_ref[0] + core, inner) * stride + at, 128)


def in_vmem(shape, dtype):
    return pltpu.VMEM(shape, dtype)


def in_hbm(x):
    return pltpu.with_memory_space_constraint(x, pltpu.MemorySpace.HBM)


def piece_copies(me, pieces, whole, out, sems):
    copies = []
    for i, piece in enumerate(pieces):
        here = pl.ds(column(me, piece), piece[-1])
        for j in range(3):
            source = whole[j].at[here, :] if j == 2 else whole[j].at[:, here]
            copies.append(pltpu.make_async_copy(source, out[3 * i + j], sems.at[i, j]))
    return copies


def piece_shapes(pieces, features):
    shapes = []
    for piece in pieces:
        shapes += [in_vmem((features, piece[-1]), BF16)] * 2
        shapes += [in_vmem((piece[-1], features), BF16)]
    return shapes


def in_threes(arrays):
    return [tuple(arrays[i : i + 3]) for i in range(0, len(arrays), 3)]


def load_kernel(pieces, me, *refs):
    copies = piece_copies(me, pieces, refs[:3], refs[3:-1], refs[-1])
    for copy in copies:
        copy.start()
    for copy in copies:
        copy.wait()


def load(me, pieces, whole):
    outs = piece_shapes(pieces, whole[0].shape[0])
    moved = 6 * sum(piece[-1] for piece in pieces) * whole[0].shape[0]
    return in_threes(
        pl.pallas_call(
            functools.partial(load_kernel, pieces),
            in_specs=[SMEM_SPEC] + [HBM_SPEC] * 3,
            out_specs=[VMEM_SPEC] * len(outs),
            out_shape=outs,
            scratch_shapes=[pltpu.SemaphoreType.DMA((len(pieces), 3))],
            compiler_params=params(),
            cost_estimate=cost(0, moved),
            name="load_weights",
        )(me, *whole)
    )


def pack_kernel(tokens, cot, packed, sems):
    rows = tokens.shape[0]
    copies = [
        pltpu.make_async_copy(tokens, packed.at[:rows], sems.at[0]),
        pltpu.make_async_copy(cot, packed.at[rows:], sems.at[1]),
    ]
    for copy in copies:
        copy.start()
    for copy in copies:
        copy.wait()


def pack(tokens, cot):
    return pl.pallas_call(
        pack_kernel,
        in_specs=[ANY_SPEC] * 2,
        out_specs=VMEM_SPEC,
        out_shape=in_vmem((2 * tokens.shape[0], tokens.shape[1]), BF16),
        scratch_shapes=[pltpu.SemaphoreType.DMA((2,))],
        compiler_params=params(),
        cost_estimate=cost(0, 8 * tokens.size),
        name="pack_rows",
    )(in_hbm(tokens), in_hbm(cot))


def forward_kernel(rows, pieces, ahead, out_dtype, count, assemble, me, *refs):
    refs = list(refs)
    take = lambda n: [refs.pop(0) for _ in range(n)]
    acts, weights = take(count), in_threes(take(3 * len(pieces)))
    whole = take(3 if ahead else 0)
    (sums,) = take(1)
    tokens_ref, cot_ref = take(2) if assemble else acts
    copies = []
    if ahead:
        out = take(3 * len(ahead))
        copies = piece_copies(me, ahead, whole, out, *take(1))
    for copy in copies:
        copy.start()

    def compute():
        if assemble:
            for k, piece in enumerate(acts):
                tokens_ref[pl.ds(k * rows, rows), :] = piece[:rows, :]
                cot_ref[pl.ds(k * rows, rows), :] = piece[rows:, :]
        tokens, cot = tokens_ref[...], cot_ref[...]
        first = 0
        for (w_gate, w_up, w_down), piece in zip(weights, pieces):
            tile = tile_of(piece[-1])
            for start in range(0, piece[-1], tile):
                here = slice(start, start + tile)
                there = slice(first, first + tile)
                first += tile
                sums[0, :, there] = contract(tokens, w_gate[:, here], 1, 0).astype(out_dtype)
                sums[1, :, there] = contract(tokens, w_up[:, here], 1, 0).astype(out_dtype)
                sums[2, :, there] = contract(cot, w_down[here, :], 1, 1).astype(out_dtype)

    if ahead:
        pl.when(me[0] >= 0)(compute)
    else:
        compute()
    for copy in copies:
        copy.wait()


def forward(me, pieces, acts, weights, rows, out_dtype, ahead, whole):
    assemble = len(acts) != 2
    features = acts[0].shape[1]
    width = sum(piece[-1] for piece in pieces)
    total = rows * len(acts) if assemble else acts[0].shape[0]
    whole = whole if ahead else ()
    outs = [in_vmem((3, total, width), out_dtype)]
    if assemble:
        outs += [in_vmem((total, features), BF16)] * 2
    outs += piece_shapes(ahead, features)
    out = pl.pallas_call(
        functools.partial(
            forward_kernel, rows, pieces, ahead, out_dtype, len(acts), assemble
        ),
        in_specs=[SMEM_SPEC]
        + [VMEM_SPEC] * (len(acts) + 3 * len(pieces))
        + [HBM_SPEC] * len(whole),
        out_specs=[VMEM_SPEC] * len(outs),
        out_shape=outs,
        scratch_shapes=[pltpu.SemaphoreType.DMA((len(ahead), 3))] * bool(ahead),
        compiler_params=params(),
        cost_estimate=cost(6 * total * width, 6 * total * width),
        name="partial_sums",
    )(me, *acts, *(x for three in weights for x in three), *whole)
    loaded = in_threes(out[len(out) - 3 * len(ahead) :]) if ahead else []
    return out[0], out[1:3] if assemble else acts, loaded


def join_kernel(mine, received, kept, sent):
    total = mine[...] + received[...].astype(F32)
    kept[...] = total
    sent[...] = total.astype(BF16)


def join(mine, received):
    return pl.pallas_call(
        join_kernel,
        in_specs=[VMEM_SPEC] * 2,
        out_specs=[VMEM_SPEC] * 2,
        out_shape=[in_vmem(mine.shape, F32), in_vmem(mine.shape, BF16)],
        compiler_params=params(),
        cost_estimate=cost(mine.size, 12 * mine.size),
        name="join_cores",
    )(mine, received)


def activate_kernel(*refs):
    kept, received, out = refs[0], refs[1:-1], refs[-1]
    gate, up, upstream = [
        sum((r[i].astype(F32) for r in received), kept[i]) for i in range(3)
    ]
    sigmoid = 1.0 / (1.0 + jnp.exp(-gate))
    swish = gate * sigmoid
    out[0] = (swish * up).astype(BF16)
    out[1] = (upstream * up * sigmoid * (1.0 + gate * (1.0 - sigmoid))).astype(BF16)
    out[2] = (upstream * swish).astype(BF16)


def activate(kept, received):
    return pl.pallas_call(
        activate_kernel,
        in_specs=[VMEM_SPEC] * (1 + len(received)),
        out_specs=VMEM_SPEC,
        out_shape=in_vmem(kept.shape, BF16),
        compiler_params=params(),
        cost_estimate=cost(8 * kept.size, 8 * kept.size),
        name="activation",
    )(kept, *received)


def backward_kernel(where, rows, grads, first, fresh, last, me, *refs):
    refs = list(refs)
    take = lambda n: [refs.pop(0) for _ in range(n)]
    acts = take(len(where))
    weights = [in_threes(take(3 * len(p))) if rows else [None] * len(p) for p in where]
    tokens, cot = take(2) if grads else (None, None)
    before = take(2) if rows and not first else None
    if grads and not fresh:
        take(3)
    sums = take(1 + last if last else 2) if rows else None
    outs = take(3) if grads else None
    out_acc, grad_acc = (take(2) if last else sums) if rows else (None, None)
    if grads:
        wide, tall, sems = take(3)
    slots = sems.shape[0] if grads else 1

    def copies(slot, at, tile):
        here = pl.ds(at, tile)
        cols = pl.ds(0, tile)
        return [
            pltpu.make_async_copy(
                wide.at[slot, 0, :, cols], outs[0].at[:, here], sems.at[slot, 0]
            ),
            pltpu.make_async_copy(
                wide.at[slot, 1, :, cols], outs[1].at[:, here], sems.at[slot, 1]
            ),
            pltpu.make_async_copy(tall.at[slot, cols], outs[2].at[here, :], sems.at[slot, 2]),
        ]

    if rows:
        if first:
            out_acc[...] = jnp.zeros_like(out_acc)
            grad_acc[...] = jnp.zeros_like(grad_acc)
        else:
            out_acc[...] = before[0][...]
            grad_acc[...] = before[1][...]
    flying, tiles = [], []
    for p, pieces in enumerate(where):
        done = 0
        for three, piece in zip(weights[p], pieces):
            tile = tile_of(piece[-1])
            for at in range(0, piece[-1], tile):
                tiles.append((p, slice(done + at, done + at + tile), three, piece, at))
            done += piece[-1]

    def make_grads(p, units, _, piece, at):
        hidden, grad_gate, grad_up = [acts[p][i, :, units] for i in range(3)]
        slot, tile = len(flying) % slots, units.stop - units.start
        if len(flying) >= slots:
            for copy in flying[len(flying) - slots]:
                copy.wait()
        cols = slice(0, tile)
        wide[slot, 0, :, cols] = contract(tokens[...], grad_gate, 0, 0).astype(BF16)
        wide[slot, 1, :, cols] = contract(tokens[...], grad_up, 0, 0).astype(BF16)
        tall[slot, cols] = contract(hidden, cot[...], 0, 0).astype(BF16)
        flying.append(copies(slot, pl.multiple_of(column(me, piece) + at, 128), tile))
        for copy in flying[-1]:
            copy.start()

    def add_rows(p, units, three, piece, at):
        hidden, grad_gate, grad_up = [acts[p][i, :, units] for i in range(3)]
        w_gate, w_up, w_down = three
        here = slice(at, at + units.stop - units.start)
        out_acc[...] += contract(hidden, w_down[here, :], 1, 0)
        grad_acc[...] += contract(grad_gate, w_gate[:, here], 1, 1) + contract(
            grad_up, w_up[:, here], 1, 1
        )

    behind = 2 if grads else 0
    for i in range(len(tiles) + behind):
        if grads and i < len(tiles) and tiles[i][0] in grads:
            make_grads(*tiles[i])
        if rows and i >= behind:
            add_rows(*tiles[i - behind])
    if last:
        n = sums[0].shape[0] // 2
        for k, ref in enumerate(sums):
            ref[:n, :] = out_acc[k * n : (k + 1) * n, :].astype(ref.dtype)
            ref[n:, :] = grad_acc[k * n : (k + 1) * n, :].astype(ref.dtype)
    for group in flying[-slots:]:
        for copy in group:
            copy.wait()


def backward(
    me, where, acts, weights, tokens, cot, before, grads, hidden, last_rows=0, of=None
):
    total = acts[0].shape[1]
    features = tokens.shape[1]
    width = sum(a.shape[2] for a in acts)
    rows, makes = before is not None, grads is not None
    args, specs, outs, out_specs, scratch = [me, *acts], [], [], [], []
    if rows:
        args += [x for part in weights for three in part for x in three]
    if makes:
        args += [tokens, cot]
    if rows:
        args += before
    specs = [SMEM_SPEC] + [VMEM_SPEC] * (len(args) - 1)
    aliases = {}
    if rows:
        if last_rows:
            shape = (2 * last_rows, features)
            outs += [in_vmem(shape, F32)] + [in_vmem(shape, BF16)] * (total // last_rows - 1)
            scratch += [pltpu.VMEM((total, features), F32)] * 2
        else:
            outs += [in_vmem((total, features), F32)] * 2
        out_specs += [VMEM_SPEC] * len(outs)
    if makes:
        aliases = {len(args) + i: len(outs) + i for i in range(len(grads))}
        args += grads
        specs += [HBM_SPEC] * len(grads)
        outs += [
            pltpu.HBM((features, hidden), BF16),
            pltpu.HBM((features, hidden), BF16),
            pltpu.HBM((hidden, features), BF16),
        ]
        out_specs += [HBM_SPEC] * 3
        tile = max(tile_of(piece[-1]) for part in where for piece in part)
        scratch += [
            pltpu.VMEM((SLOTS, 2, features, tile), BF16),
            pltpu.VMEM((SLOTS, tile, features), BF16),
            pltpu.SemaphoreType.DMA((SLOTS, 3)),
        ]
    work = width * features * (rows + makes)
    out = pl.pallas_call(
        functools.partial(
            backward_kernel, where, rows, of or range(len(where)) if makes else (), not before, not grads,
            total // last_rows - 1 if last_rows else 0,
        ),
        in_specs=specs,
        out_specs=out_specs,
        out_shape=outs,
        scratch_shapes=scratch,
        input_output_aliases=aliases,
        compiler_params=params(),
        cost_estimate=cost(6 * total * work, 6 * work),
        name="output_rows" if not makes else "weight_grads" if not rows else "backward",
    )(*args)
    return (out[:-3], out[-3:]) if makes else (out, None)


def finish_kernel(*refs):
    mine, received, (output, grad_input) = refs[0], refs[1:-2], refs[-2:]
    rows = output.shape[0]
    total = mine[...]
    for r in received:
        total = total + r[...].astype(F32)
    output[...] = total[:rows].astype(BF16)
    grad_input[...] = total[rows:].astype(BF16)


def finish(mine, received):
    shape = jax.ShapeDtypeStruct((mine.shape[0] // 2, mine.shape[1]), BF16)
    return pl.pallas_call(
        finish_kernel,
        in_specs=[VMEM_SPEC] * (1 + len(received)),
        out_specs=[VMEM_SPEC] * 2,
        out_shape=[shape] * 2,
        compiler_params=params(),
        name="finish_rows",
    )(mine, *received)


def chunk_parts(hidden, inner):
    units = hidden // inner
    if units % 2048 == 0:
        chunks = [[units * share // 16 for share in chunk] for chunk in CHUNKS]
    else:
        chunks = [[units // 2]] * 2 if units % 256 == 0 else [[units]]
    parts, start = [], 0
    for widths in chunks:
        stride = sum(widths)
        parts.append([
            [(start, core, inner, stride, sum(widths[:i]), w) for i, w in enumerate(widths)]
            for core in range(inner)
        ])
        start += inner * stride
    return parts


def tied(acts, held):
    acts, arrays = lax.optimization_barrier((acts, list(held.values())))
    return acts, dict(zip(held, arrays))


def body(sizes, tokens, cotangent, w_gate, w_up, w_down):
    wide, narrow, inner = sizes["wide"], sizes["narrow"], sizes["inner"]
    rows = tokens.shape[0]
    hidden = w_gate.shape[1]
    me = lax.axis_index("inner").astype(jnp.int32).reshape(1)
    parts = chunk_parts(hidden, inner)
    whole = tuple(in_hbm(w) for w in (w_gate, w_up, w_down))

    packed = pack(tokens, cotangent)
    acts = [packed] + [shift(packed, "wide", wide, k) for k in range(1, wide)]
    uses = [pieces for mine, other in parts for pieces in (other, mine)]
    queue = [piece for pieces in uses for piece in pieces]
    plan, seen = [[]], 0
    while queue and (not plan[0] or 2 * (seen + queue[0][-1]) <= hidden):
        seen += queue[0][-1]
        plan[0].append(queue.pop(0))
    for i in range(len(uses)):
        plan.append([queue.pop(0)] if queue else [])
        while queue and i + 1 < len(uses) and queue[0] in uses[i + 1]:
            plan[-1].append(queue.pop(0))
    held = dict(zip(plan[0], load(me, plan[0], whole)))
    acts, held = tied(acts, held)
    kept, products, crossed = [], [], []
    step = 1
    for mine, other in parts:
        made = []
        for pieces, dtype in ((other, BF16), (mine, F32)):
            weights = [held[piece] for piece in pieces]
            out, acts, loaded = forward(
                me, pieces, acts, weights, rows, dtype, plan[step], whole
            )
            held.update(zip(plan[step], loaded))
            step += 1
            made.append(out)
        products.append(made)
        total, out = join(made[1], shift(made[0], "inner", inner, 1))
        acts, _ = lax.optimization_barrier((acts, out))
        kept.append(total)
        crossed.append([shift(out, "narrow", narrow, k) for k in range(1, narrow)])
    tokens_all, cot_all = acts
    crossed[0], _ = lax.optimization_barrier((crossed[0], products[-1]))
    sums, grads, later = (), (), []
    for i, where in enumerate(parts):
        own = activate(kept[i], crossed[i])
        acts = [own, shift(own, "inner", inner, 1)]
        weights = [[held[piece] for piece in pieces] for pieces in where]
        if where is parts[-1]:
            later += list(zip(where, acts))
        else:
            of = (0, 1)
            if i == len(parts) - 2 and i:
                of, later = (0,), [(where[1], acts[1])]
            sums, grads = backward(
                me, where, acts, weights, tokens_all, cot_all, sums, grads, hidden, of=of
            )
            crossed[i + 1], sums = lax.optimization_barrier((crossed[i + 1], sums))
    for last, (pieces, act, three) in enumerate(zip(where, acts, weights)):
        sums, _ = backward(
            me, [pieces], [act], [three], tokens_all, cot_all, sums, None, hidden,
            rows if last else 0,
        )
    back = [shift(sums[k], "wide", wide, -k) for k in range(1, wide)]
    where, acts = zip(*later)
    _, grads = backward(me, where, acts, None, tokens_all, cot_all, None, grads, hidden)
    output, grad_input = finish(sums[0], back)
    return (output, grad_input, *grads)


def solution(mesh):
    rows = P(("groups", "wide"), ("narrow", "inner"))
    return jax.shard_map(
        functools.partial(body, dict(mesh.shape)),
        mesh=mesh,
        in_specs=(
            rows,
            rows,
            P(("narrow", "inner"), "wide"),
            P(("narrow", "inner"), "wide"),
            P("wide", ("narrow", "inner")),
        ),
        out_specs=(
            rows,
            rows,
            P(("groups", "narrow", "inner"), "wide"),
            P(("groups", "narrow", "inner"), "wide"),
            P(("groups", "wide"), ("narrow", "inner")),
        ),
        check_vma=False,
    )
```

```python
import functools

import jax
import jax.numpy as jnp
from jax import lax
from jax.experimental import pallas as pl
from jax.experimental.pallas import tpu as pltpu
from jax.sharding import PartitionSpec as P

F32 = jnp.float32
BF16 = jnp.bfloat16
CHUNKS = ((8,), (4, 4))
VMEM_SPEC = pl.BlockSpec(memory_space=pltpu.VMEM)
SMEM_SPEC = pl.BlockSpec(memory_space=pltpu.SMEM)
ANY_SPEC = pl.BlockSpec(memory_space=pl.ANY)
HBM_SPEC = pl.BlockSpec(memory_space=pltpu.MemorySpace.HBM)
LIMIT = 10 << 20
SLOTS = 3


def contract(left, right, left_dim, right_dim):
    return lax.dot_general(
        left, right, (((left_dim,), (right_dim,)), ((), ())), preferred_element_type=F32
    )


def tile_of(width):
    return 256 if width % 256 == 0 else 128


def params(**more):
    return pltpu.CompilerParams(vmem_limit_bytes=LIMIT, **more)


def cost(flops, moved):
    return pl.CostEstimate(flops=int(flops), bytes_accessed=int(moved), transcendentals=0)


def shift(x, axis, size, by):
    return lax.ppermute(x, axis, [(i, (i + by) % size) for i in range(size)])


def column(me_ref, piece):
    start, core, inner, stride, at, _ = piece
    return pl.multiple_of(start + lax.rem(me_ref[0] + core, inner) * stride + at, 128)


def in_vmem(shape, dtype):
    return pltpu.VMEM(shape, dtype)


def in_hbm(x):
    return pltpu.with_memory_space_constraint(x, pltpu.MemorySpace.HBM)


def piece_copies(me, pieces, whole, out, sems):
    copies = []
    for i, piece in enumerate(pieces):
        here = pl.ds(column(me, piece), piece[-1])
        for j in range(3):
            source = whole[j].at[here, :] if j == 2 else whole[j].at[:, here]
            copies.append(pltpu.make_async_copy(source, out[3 * i + j], sems.at[i, j]))
    return copies


def piece_shapes(pieces, features):
    shapes = []
    for piece in pieces:
        shapes += [in_vmem((features, piece[-1]), BF16)] * 2
        shapes += [in_vmem((piece[-1], features), BF16)]
    return shapes


def in_threes(arrays):
    return [tuple(arrays[i : i + 3]) for i in range(0, len(arrays), 3)]


def load_kernel(pieces, me, *refs):
    copies = piece_copies(me, pieces, refs[:3], refs[3:-1], refs[-1])
    for copy in copies:
        copy.start()
    for copy in copies:
        copy.wait()


def load(me, pieces, whole):
    outs = piece_shapes(pieces, whole[0].shape[0])
    moved = 6 * sum(piece[-1] for piece in pieces) * whole[0].shape[0]
    return in_threes(
        pl.pallas_call(
            functools.partial(load_kernel, pieces),
            in_specs=[SMEM_SPEC] + [HBM_SPEC] * 3,
            out_specs=[VMEM_SPEC] * len(outs),
            out_shape=outs,
            scratch_shapes=[pltpu.SemaphoreType.DMA((len(pieces), 3))],
            compiler_params=params(),
            cost_estimate=cost(0, moved),
            name="load_weights",
        )(me, *whole)
    )


def pack_kernel(tokens, cot, packed, sems):
    rows = tokens.shape[0]
    copies = [
        pltpu.make_async_copy(tokens, packed.at[:rows], sems.at[0]),
        pltpu.make_async_copy(cot, packed.at[rows:], sems.at[1]),
    ]
    for copy in copies:
        copy.start()
    for copy in copies:
        copy.wait()


def pack(tokens, cot):
    return pl.pallas_call(
        pack_kernel,
        in_specs=[ANY_SPEC] * 2,
        out_specs=VMEM_SPEC,
        out_shape=in_vmem((2 * tokens.shape[0], tokens.shape[1]), BF16),
        scratch_shapes=[pltpu.SemaphoreType.DMA((2,))],
        compiler_params=params(),
        cost_estimate=cost(0, 8 * tokens.size),
        name="pack_rows",
    )(in_hbm(tokens), in_hbm(cot))


def forward_kernel(rows, pieces, ahead, out_dtype, count, assemble, me, *refs):
    refs = list(refs)
    take = lambda n: [refs.pop(0) for _ in range(n)]
    acts, weights = take(count), in_threes(take(3 * len(pieces)))
    whole = take(3 if ahead else 0)
    (sums,) = take(1)
    tokens_ref, cot_ref = take(2) if assemble else acts
    copies = []
    if ahead:
        out = take(3 * len(ahead))
        copies = piece_copies(me, ahead, whole, out, *take(1))
    for copy in copies:
        copy.start()

    def compute():
        if assemble:
            for k, piece in enumerate(acts):
                tokens_ref[pl.ds(k * rows, rows), :] = piece[:rows, :]
                cot_ref[pl.ds(k * rows, rows), :] = piece[rows:, :]
        tokens, cot = tokens_ref[...], cot_ref[...]
        first = 0
        for (w_gate, w_up, w_down), piece in zip(weights, pieces):
            tile = tile_of(piece[-1])
            for start in range(0, piece[-1], tile):
                here = slice(start, start + tile)
                there = slice(first, first + tile)
                first += tile
                sums[0, :, there] = contract(tokens, w_gate[:, here], 1, 0).astype(out_dtype)
                sums[1, :, there] = contract(tokens, w_up[:, here], 1, 0).astype(out_dtype)
                sums[2, :, there] = contract(cot, w_down[here, :], 1, 1).astype(out_dtype)

    if ahead:
        pl.when(me[0] >= 0)(compute)
    else:
        compute()
    for copy in copies:
        copy.wait()


def forward(me, pieces, acts, weights, rows, out_dtype, ahead, whole):
    assemble = len(acts) != 2
    features = acts[0].shape[1]
    width = sum(piece[-1] for piece in pieces)
    total = rows * len(acts) if assemble else acts[0].shape[0]
    whole = whole if ahead else ()
    outs = [in_vmem((3, total, width), out_dtype)]
    if assemble:
        outs += [in_vmem((total, features), BF16)] * 2
    outs += piece_shapes(ahead, features)
    out = pl.pallas_call(
        functools.partial(
            forward_kernel, rows, pieces, ahead, out_dtype, len(acts), assemble
        ),
        in_specs=[SMEM_SPEC]
        + [VMEM_SPEC] * (len(acts) + 3 * len(pieces))
        + [HBM_SPEC] * len(whole),
        out_specs=[VMEM_SPEC] * len(outs),
        out_shape=outs,
        scratch_shapes=[pltpu.SemaphoreType.DMA((len(ahead), 3))] * bool(ahead),
        compiler_params=params(),
        cost_estimate=cost(6 * total * width, 6 * total * width),
        name="partial_sums",
    )(me, *acts, *(x for three in weights for x in three), *whole)
    loaded = in_threes(out[len(out) - 3 * len(ahead) :]) if ahead else []
    return out[0], out[1:3] if assemble else acts, loaded


def join_kernel(mine, received, kept, sent):
    total = mine[...] + received[...].astype(F32)
    kept[...] = total
    sent[...] = total.astype(BF16)


def join(mine, received):
    return pl.pallas_call(
        join_kernel,
        in_specs=[VMEM_SPEC] * 2,
        out_specs=[VMEM_SPEC] * 2,
        out_shape=[in_vmem(mine.shape, F32), in_vmem(mine.shape, BF16)],
        compiler_params=params(),
        cost_estimate=cost(mine.size, 12 * mine.size),
        name="join_cores",
    )(mine, received)


def activate_kernel(*refs):
    kept, received, out = refs[0], refs[1:-1], refs[-1]
    gate, up, upstream = [
        sum((r[i].astype(F32) for r in received), kept[i]) for i in range(3)
    ]
    sigmoid = 1.0 / (1.0 + jnp.exp(-gate))
    swish = gate * sigmoid
    out[0] = (swish * up).astype(BF16)
    out[1] = (upstream * up * sigmoid * (1.0 + gate * (1.0 - sigmoid))).astype(BF16)
    out[2] = (upstream * swish).astype(BF16)


def activate(kept, received):
    return pl.pallas_call(
        activate_kernel,
        in_specs=[VMEM_SPEC] * (1 + len(received)),
        out_specs=VMEM_SPEC,
        out_shape=in_vmem(kept.shape, BF16),
        compiler_params=params(),
        cost_estimate=cost(8 * kept.size, 8 * kept.size),
        name="activation",
    )(kept, *received)


def backward_kernel(where, rows, grads, first, fresh, last, me, *refs):
    refs = list(refs)
    take = lambda n: [refs.pop(0) for _ in range(n)]
    acts = take(len(where))
    weights = [in_threes(take(3 * len(p))) if rows else [None] * len(p) for p in where]
    tokens, cot = take(2) if grads else (None, None)
    before = take(2) if rows and not first else None
    if grads and not fresh:
        take(3)
    sums = take(1 + last if last else 2) if rows else None
    outs = take(3) if grads else None
    out_acc, grad_acc = (take(2) if last else sums) if rows else (None, None)
    if grads:
        wide, tall, sems = take(3)
    slots = sems.shape[0] if grads else 1

    def copies(slot, at, tile):
        here = pl.ds(at, tile)
        cols = pl.ds(0, tile)
        return [
            pltpu.make_async_copy(
                wide.at[slot, 0, :, cols], outs[0].at[:, here], sems.at[slot, 0]
            ),
            pltpu.make_async_copy(
                wide.at[slot, 1, :, cols], outs[1].at[:, here], sems.at[slot, 1]
            ),
            pltpu.make_async_copy(tall.at[slot, cols], outs[2].at[here, :], sems.at[slot, 2]),
        ]

    if rows:
        if first:
            out_acc[...] = jnp.zeros_like(out_acc)
            grad_acc[...] = jnp.zeros_like(grad_acc)
        else:
            out_acc[...] = before[0][...]
            grad_acc[...] = before[1][...]
    flying, tiles = [], []
    for p, pieces in enumerate(where):
        done = 0
        for three, piece in zip(weights[p], pieces):
            tile = tile_of(piece[-1])
            for at in range(0, piece[-1], tile):
                tiles.append((p, slice(done + at, done + at + tile), three, piece, at))
            done += piece[-1]

    def make_grads(p, units, _, piece, at):
        hidden, grad_gate, grad_up = [acts[p][i, :, units] for i in range(3)]
        slot, tile = len(flying) % slots, units.stop - units.start
        if len(flying) >= slots:
            for copy in flying[len(flying) - slots]:
                copy.wait()
        cols = slice(0, tile)
        wide[slot, 0, :, cols] = contract(tokens[...], grad_gate, 0, 0).astype(BF16)
        wide[slot, 1, :, cols] = contract(tokens[...], grad_up, 0, 0).astype(BF16)
        tall[slot, cols] = contract(hidden, cot[...], 0, 0).astype(BF16)
        flying.append(copies(slot, pl.multiple_of(column(me, piece) + at, 128), tile))
        for copy in flying[-1]:
            copy.start()

    def add_rows(p, units, three, piece, at):
        hidden, grad_gate, grad_up = [acts[p][i, :, units] for i in range(3)]
        w_gate, w_up, w_down = three
        here = slice(at, at + units.stop - units.start)
        out_acc[...] += contract(hidden, w_down[here, :], 1, 0)
        grad_acc[...] += contract(grad_gate, w_gate[:, here], 1, 1) + contract(
            grad_up, w_up[:, here], 1, 1
        )

    behind = 2 if grads else 0
    for i in range(len(tiles) + behind):
        if grads and i < len(tiles) and tiles[i][0] in grads:
            make_grads(*tiles[i])
        if rows and i >= behind:
            add_rows(*tiles[i - behind])
    if last:
        n = sums[0].shape[0] // 2
        for k, ref in enumerate(sums):
            ref[:n, :] = out_acc[k * n : (k + 1) * n, :].astype(ref.dtype)
            ref[n:, :] = grad_acc[k * n : (k + 1) * n, :].astype(ref.dtype)
    for group in flying[-slots:]:
        for copy in group:
            copy.wait()


def backward(
    me, where, acts, weights, tokens, cot, before, grads, hidden, last_rows=0, of=None
):
    total = acts[0].shape[1]
    features = tokens.shape[1]
    width = sum(a.shape[2] for a in acts)
    rows, makes = before is not None, grads is not None
    args, specs, outs, out_specs, scratch = [me, *acts], [], [], [], []
    if rows:
        args += [x for part in weights for three in part for x in three]
    if makes:
        args += [tokens, cot]
    if rows:
        args += before
    specs = [SMEM_SPEC] + [VMEM_SPEC] * (len(args) - 1)
    aliases = {}
    if rows:
        if last_rows:
            shape = (2 * last_rows, features)
            outs += [in_vmem(shape, F32)] + [in_vmem(shape, BF16)] * (total // last_rows - 1)
            scratch += [pltpu.VMEM((total, features), F32)] * 2
        else:
            outs += [in_vmem((total, features), F32)] * 2
        out_specs += [VMEM_SPEC] * len(outs)
    if makes:
        aliases = {len(args) + i: len(outs) + i for i in range(len(grads))}
        args += grads
        specs += [HBM_SPEC] * len(grads)
        outs += [
            pltpu.HBM((features, hidden), BF16),
            pltpu.HBM((features, hidden), BF16),
            pltpu.HBM((hidden, features), BF16),
        ]
        out_specs += [HBM_SPEC] * 3
        tile = max(tile_of(piece[-1]) for part in where for piece in part)
        scratch += [
            pltpu.VMEM((SLOTS, 2, features, tile), BF16),
            pltpu.VMEM((SLOTS, tile, features), BF16),
            pltpu.SemaphoreType.DMA((SLOTS, 3)),
        ]
    work = width * features * (rows + makes)
    out = pl.pallas_call(
        functools.partial(
            backward_kernel, where, rows, of or range(len(where)) if makes else (), not before, not grads,
            total // last_rows - 1 if last_rows else 0,
        ),
        in_specs=specs,
        out_specs=out_specs,
        out_shape=outs,
        scratch_shapes=scratch,
        input_output_aliases=aliases,
        compiler_params=params(),
        cost_estimate=cost(6 * total * work, 6 * work),
        name="output_rows" if not makes else "weight_grads" if not rows else "backward",
    )(*args)
    return (out[:-3], out[-3:]) if makes else (out, None)


def finish_kernel(*refs):
    mine, received, (output, grad_input) = refs[0], refs[1:-2], refs[-2:]
    rows = output.shape[0]
    total = mine[...]
    for r in received:
        total = total + r[...].astype(F32)
    output[...] = total[:rows].astype(BF16)
    grad_input[...] = total[rows:].astype(BF16)


def finish(mine, received):
    shape = jax.ShapeDtypeStruct((mine.shape[0] // 2, mine.shape[1]), BF16)
    return pl.pallas_call(
        finish_kernel,
        in_specs=[VMEM_SPEC] * (1 + len(received)),
        out_specs=[VMEM_SPEC] * 2,
        out_shape=[shape] * 2,
        compiler_params=params(),
        name="finish_rows",
    )(mine, *received)


def chunk_parts(hidden, inner):
    units = hidden // inner
    if units % 2048 == 0:
        chunks = [[units * share // 16 for share in chunk] for chunk in CHUNKS]
    else:
        chunks = [[units // 2]] * 2 if units % 256 == 0 else [[units]]
    parts, start = [], 0
    for widths in chunks:
        stride = sum(widths)
        parts.append([
            [(start, core, inner, stride, sum(widths[:i]), w) for i, w in enumerate(widths)]
            for core in range(inner)
        ])
        start += inner * stride
    return parts


def tied(acts, held):
    acts, arrays = lax.optimization_barrier((acts, list(held.values())))
    return acts, dict(zip(held, arrays))


def body(sizes, tokens, cotangent, w_gate, w_up, w_down):
    wide, narrow, inner = sizes["wide"], sizes["narrow"], sizes["inner"]
    rows = tokens.shape[0]
    hidden = w_gate.shape[1]
    me = lax.axis_index("inner").astype(jnp.int32).reshape(1)
    parts = chunk_parts(hidden, inner)
    whole = tuple(in_hbm(w) for w in (w_gate, w_up, w_down))

    packed = pack(tokens, cotangent)
    acts = [packed] + [shift(packed, "wide", wide, k) for k in range(1, wide)]
    uses = [pieces for mine, other in parts for pieces in (other, mine)]
    queue = [piece for pieces in uses for piece in pieces]
    plan, seen = [[]], 0
    while queue and (not plan[0] or 2 * (seen + queue[0][-1]) <= hidden):
        seen += queue[0][-1]
        plan[0].append(queue.pop(0))
    for i in range(len(uses)):
        plan.append([queue.pop(0)] if queue else [])
        while queue and i + 1 < len(uses) and queue[0] in uses[i + 1]:
            plan[-1].append(queue.pop(0))
    held = dict(zip(plan[0], load(me, plan[0], whole)))
    acts, held = tied(acts, held)
    kept, products, crossed = [], [], []
    step = 1
    for mine, other in parts:
        made = []
        for pieces, dtype in ((other, BF16), (mine, F32)):
            weights = [held[piece] for piece in pieces]
            out, acts, loaded = forward(
                me, pieces, acts, weights, rows, dtype, plan[step], whole
            )
            held.update(zip(plan[step], loaded))
            step += 1
            made.append(out)
        products.append(made)
        total, out = join(made[1], shift(made[0], "inner", inner, 1))
        acts, _ = lax.optimization_barrier((acts, out))
        kept.append(total)
        crossed.append([shift(out, "narrow", narrow, k) for k in range(1, narrow)])
    tokens_all, cot_all = acts
    crossed[0], _ = lax.optimization_barrier((crossed[0], products[-1]))
    sums, grads, later = (), (), []
    for i, where in enumerate(parts):
        own = activate(kept[i], crossed[i])
        acts = [own, shift(own, "inner", inner, 1)]
        weights = [[held[piece] for piece in pieces] for pieces in where]
        if where is parts[-1]:
            later += list(zip(where, acts))
        else:
            of = (0, 1)
            if i == len(parts) - 2 and i:
                of, later = (0,), [(where[1], acts[1])]
            sums, grads = backward(
                me, where, acts, weights, tokens_all, cot_all, sums, grads, hidden, of=of
            )
            crossed[i + 1], sums = lax.optimization_barrier((crossed[i + 1], sums))
    for last, (pieces, act, three) in enumerate(zip(where, acts, weights)):
        sums, _ = backward(
            me, [pieces], [act], [three], tokens_all, cot_all, sums, None, hidden,
            rows if last else 0,
        )
    back = [shift(sums[k], "wide", wide, -k) for k in range(1, wide)]
    where, acts = zip(*later)
    _, grads = backward(me, where, acts, None, tokens_all, cot_all, None, grads, hidden)
    output, grad_input = finish(sums[0], back)
    return (output, grad_input, *grads)


def solution(mesh):
    rows = P(("groups", "wide"), ("narrow", "inner"))
    return jax.shard_map(
        functools.partial(body, dict(mesh.shape)),
        mesh=mesh,
        in_specs=(
            rows,
            rows,
            P(("narrow", "inner"), "wide"),
            P(("narrow", "inner"), "wide"),
            P("wide", ("narrow", "inner")),
        ),
        out_specs=(
            rows,
            rows,
            P(("groups", "narrow", "inner"), "wide"),
            P(("groups", "narrow", "inner"), "wide"),
            P(("groups", "wide"), ("narrow", "inner")),
        ),
        check_vma=False,
    )
```

```python
import functools

import jax
import jax.numpy as jnp
from jax import lax
from jax.experimental import pallas as pl
from jax.experimental.pallas import tpu as pltpu
from jax.sharding import PartitionSpec as P

F32 = jnp.float32
BF16 = jnp.bfloat16
CHUNKS = ((4, 4), (4, 4))
VMEM_SPEC = pl.BlockSpec(memory_space=pltpu.VMEM)
SMEM_SPEC = pl.BlockSpec(memory_space=pltpu.SMEM)
ANY_SPEC = pl.BlockSpec(memory_space=pl.ANY)
HBM_SPEC = pl.BlockSpec(memory_space=pltpu.MemorySpace.HBM)
LIMIT = 10 << 20
SLOTS = 3


def contract(left, right, left_dim, right_dim):
    return lax.dot_general(
        left, right, (((left_dim,), (right_dim,)), ((), ())), preferred_element_type=F32
    )


def tile_of(width):
    return 256 if width % 256 == 0 else 128


def params(**more):
    return pltpu.CompilerParams(vmem_limit_bytes=LIMIT, **more)


def cost(flops, moved):
    return pl.CostEstimate(flops=int(flops), bytes_accessed=int(moved), transcendentals=0)


def shift(x, axis, size, by):
    return lax.ppermute(x, axis, [(i, (i + by) % size) for i in range(size)])


def column(me_ref, piece):
    start, core, inner, stride, at, _ = piece
    return pl.multiple_of(start + lax.rem(me_ref[0] + core, inner) * stride + at, 128)


def in_vmem(shape, dtype):
    return pltpu.VMEM(shape, dtype)


def in_hbm(x):
    return pltpu.with_memory_space_constraint(x, pltpu.MemorySpace.HBM)


def piece_copies(me, pieces, whole, out, sems):
    copies = []
    for i, piece in enumerate(pieces):
        here = pl.ds(column(me, piece), piece[-1])
        for j in range(3):
            source = whole[j].at[here, :] if j == 2 else whole[j].at[:, here]
            copies.append(pltpu.make_async_copy(source, out[3 * i + j], sems.at[i, j]))
    return copies


def piece_shapes(pieces, features):
    shapes = []
    for piece in pieces:
        shapes += [in_vmem((features, piece[-1]), BF16)] * 2
        shapes += [in_vmem((piece[-1], features), BF16)]
    return shapes


def in_threes(arrays):
    return [tuple(arrays[i : i + 3]) for i in range(0, len(arrays), 3)]


def load_kernel(pieces, me, *refs):
    copies = piece_copies(me, pieces, refs[:3], refs[3:-1], refs[-1])
    for copy in copies:
        copy.start()
    for copy in copies:
        copy.wait()


def load(me, pieces, whole):
    outs = piece_shapes(pieces, whole[0].shape[0])
    moved = 6 * sum(piece[-1] for piece in pieces) * whole[0].shape[0]
    return in_threes(
        pl.pallas_call(
            functools.partial(load_kernel, pieces),
            in_specs=[SMEM_SPEC] + [HBM_SPEC] * 3,
            out_specs=[VMEM_SPEC] * len(outs),
            out_shape=outs,
            scratch_shapes=[pltpu.SemaphoreType.DMA((len(pieces), 3))],
            compiler_params=params(),
            cost_estimate=cost(0, moved),
            name="load_weights",
        )(me, *whole)
    )


def pack_kernel(tokens, cot, packed, sems):
    rows = tokens.shape[0]
    copies = [
        pltpu.make_async_copy(tokens, packed.at[:rows], sems.at[0]),
        pltpu.make_async_copy(cot, packed.at[rows:], sems.at[1]),
    ]
    for copy in copies:
        copy.start()
    for copy in copies:
        copy.wait()


def pack(tokens, cot):
    return pl.pallas_call(
        pack_kernel,
        in_specs=[ANY_SPEC] * 2,
        out_specs=VMEM_SPEC,
        out_shape=in_vmem((2 * tokens.shape[0], tokens.shape[1]), BF16),
        scratch_shapes=[pltpu.SemaphoreType.DMA((2,))],
        compiler_params=params(),
        cost_estimate=cost(0, 8 * tokens.size),
        name="pack_rows",
    )(in_hbm(tokens), in_hbm(cot))


def forward_kernel(rows, pieces, ahead, out_dtype, count, assemble, me, *refs):
    refs = list(refs)
    take = lambda n: [refs.pop(0) for _ in range(n)]
    acts, weights = take(count), in_threes(take(3 * len(pieces)))
    whole = take(3 if ahead else 0)
    (sums,) = take(1)
    tokens_ref, cot_ref = take(2) if assemble else acts
    copies = []
    if ahead:
        out = take(3 * len(ahead))
        copies = piece_copies(me, ahead, whole, out, *take(1))
    for copy in copies:
        copy.start()

    def compute():
        if assemble:
            for k, piece in enumerate(acts):
                tokens_ref[pl.ds(k * rows, rows), :] = piece[:rows, :]
                cot_ref[pl.ds(k * rows, rows), :] = piece[rows:, :]
        tokens, cot = tokens_ref[...], cot_ref[...]
        first = 0
        for (w_gate, w_up, w_down), piece in zip(weights, pieces):
            tile = tile_of(piece[-1])
            for start in range(0, piece[-1], tile):
                here = slice(start, start + tile)
                there = slice(first, first + tile)
                first += tile
                sums[0, :, there] = contract(tokens, w_gate[:, here], 1, 0).astype(out_dtype)
                sums[1, :, there] = contract(tokens, w_up[:, here], 1, 0).astype(out_dtype)
                sums[2, :, there] = contract(cot, w_down[here, :], 1, 1).astype(out_dtype)

    if ahead:
        pl.when(me[0] >= 0)(compute)
    else:
        compute()
    for copy in copies:
        copy.wait()


def forward(me, pieces, acts, weights, rows, out_dtype, ahead, whole):
    assemble = len(acts) != 2
    features = acts[0].shape[1]
    width = sum(piece[-1] for piece in pieces)
    total = rows * len(acts) if assemble else acts[0].shape[0]
    whole = whole if ahead else ()
    outs = [in_vmem((3, total, width), out_dtype)]
    if assemble:
        outs += [in_vmem((total, features), BF16)] * 2
    outs += piece_shapes(ahead, features)
    out = pl.pallas_call(
        functools.partial(
            forward_kernel, rows, pieces, ahead, out_dtype, len(acts), assemble
        ),
        in_specs=[SMEM_SPEC]
        + [VMEM_SPEC] * (len(acts) + 3 * len(pieces))
        + [HBM_SPEC] * len(whole),
        out_specs=[VMEM_SPEC] * len(outs),
        out_shape=outs,
        scratch_shapes=[pltpu.SemaphoreType.DMA((len(ahead), 3))] * bool(ahead),
        compiler_params=params(),
        cost_estimate=cost(6 * total * width, 6 * total * width),
        name="partial_sums",
    )(me, *acts, *(x for three in weights for x in three), *whole)
    loaded = in_threes(out[len(out) - 3 * len(ahead) :]) if ahead else []
    return out[0], out[1:3] if assemble else acts, loaded


def join_kernel(mine, received, *outs):
    first = 0
    for kept, sent in zip(outs[0::2], outs[1::2]):
        here = slice(first, first + kept.shape[2])
        first += kept.shape[2]
        total = mine[:, :, here] + received[:, :, here].astype(F32)
        kept[...] = total
        sent[...] = total.astype(BF16)


def join(mine, received, widths):
    outs = []
    for width in widths:
        outs += [in_vmem((*mine.shape[:2], width), dtype) for dtype in (F32, BF16)]
    out = pl.pallas_call(
        join_kernel,
        in_specs=[VMEM_SPEC] * 2,
        out_specs=[VMEM_SPEC] * len(outs),
        out_shape=outs,
        compiler_params=params(),
        cost_estimate=cost(mine.size, 12 * mine.size),
        name="join_cores",
    )(mine, received)
    return list(zip(out[0::2], out[1::2]))


def activate_kernel(*refs):
    kept, received, out = refs[0], refs[1:-1], refs[-1]
    gate, up, upstream = [
        sum((r[i].astype(F32) for r in received), kept[i]) for i in range(3)
    ]
    sigmoid = 1.0 / (1.0 + jnp.exp(-gate))
    swish = gate * sigmoid
    out[0] = (swish * up).astype(BF16)
    out[1] = (upstream * up * sigmoid * (1.0 + gate * (1.0 - sigmoid))).astype(BF16)
    out[2] = (upstream * swish).astype(BF16)


def activate(kept, received):
    return pl.pallas_call(
        activate_kernel,
        in_specs=[VMEM_SPEC] * (1 + len(received)),
        out_specs=VMEM_SPEC,
        out_shape=in_vmem(kept.shape, BF16),
        compiler_params=params(),
        cost_estimate=cost(8 * kept.size, 8 * kept.size),
        name="activation",
    )(kept, *received)


def backward_kernel(where, rows, grads, first, fresh, last, me, *refs):
    refs = list(refs)
    take = lambda n: [refs.pop(0) for _ in range(n)]
    acts = take(len(where))
    weights = [in_threes(take(3 * len(p))) if rows else [None] * len(p) for p in where]
    tokens, cot = take(2) if grads else (None, None)
    before = take(2) if rows and not first else None
    if grads and not fresh:
        take(3)
    sums = take(1 + last if last else 2) if rows else None
    outs = take(3) if grads else None
    out_acc, grad_acc = (take(2) if last else sums) if rows else (None, None)
    if grads:
        wide, tall, sems = take(3)
    slots = sems.shape[0] if grads else 1

    def copies(slot, at, tile):
        here = pl.ds(at, tile)
        cols = pl.ds(0, tile)
        return [
            pltpu.make_async_copy(
                wide.at[slot, 0, :, cols], outs[0].at[:, here], sems.at[slot, 0]
            ),
            pltpu.make_async_copy(
                wide.at[slot, 1, :, cols], outs[1].at[:, here], sems.at[slot, 1]
            ),
            pltpu.make_async_copy(tall.at[slot, cols], outs[2].at[here, :], sems.at[slot, 2]),
        ]

    if rows:
        if first:
            out_acc[...] = jnp.zeros_like(out_acc)
            grad_acc[...] = jnp.zeros_like(grad_acc)
        else:
            out_acc[...] = before[0][...]
            grad_acc[...] = before[1][...]
    flying, tiles = [], []
    for p, pieces in enumerate(where):
        done = 0
        for three, piece in zip(weights[p], pieces):
            tile = tile_of(piece[-1])
            for at in range(0, piece[-1], tile):
                tiles.append((p, slice(done + at, done + at + tile), three, piece, at))
            done += piece[-1]

    def make_grads(p, units, _, piece, at):
        hidden, grad_gate, grad_up = [acts[p][i, :, units] for i in range(3)]
        slot, tile = len(flying) % slots, units.stop - units.start
        if len(flying) >= slots:
            for copy in flying[len(flying) - slots]:
                copy.wait()
        cols = slice(0, tile)
        wide[slot, 0, :, cols] = contract(tokens[...], grad_gate, 0, 0).astype(BF16)
        wide[slot, 1, :, cols] = contract(tokens[...], grad_up, 0, 0).astype(BF16)
        tall[slot, cols] = contract(hidden, cot[...], 0, 0).astype(BF16)
        flying.append(copies(slot, pl.multiple_of(column(me, piece) + at, 128), tile))
        for copy in flying[-1]:
            copy.start()

    def add_rows(p, units, three, piece, at):
        hidden, grad_gate, grad_up = [acts[p][i, :, units] for i in range(3)]
        w_gate, w_up, w_down = three
        here = slice(at, at + units.stop - units.start)
        out_acc[...] += contract(hidden, w_down[here, :], 1, 0)
        grad_acc[...] += contract(grad_gate, w_gate[:, here], 1, 1) + contract(
            grad_up, w_up[:, here], 1, 1
        )

    behind = 2 if grads else 0
    for i in range(len(tiles) + behind):
        if grads and i < len(tiles) and tiles[i][0] in grads:
            make_grads(*tiles[i])
        if rows and i >= behind:
            add_rows(*tiles[i - behind])
    if last:
        n = sums[0].shape[0] // 2
        for k, ref in enumerate(sums):
            ref[:n, :] = out_acc[k * n : (k + 1) * n, :].astype(ref.dtype)
            ref[n:, :] = grad_acc[k * n : (k + 1) * n, :].astype(ref.dtype)
    for group in flying[-slots:]:
        for copy in group:
            copy.wait()


def backward(
    me, where, acts, weights, tokens, cot, before, grads, hidden, last_rows=0, of=None
):
    total = acts[0].shape[1]
    features = tokens.shape[1]
    width = sum(a.shape[2] for a in acts)
    rows, makes = before is not None, grads is not None
    args, specs, outs, out_specs, scratch = [me, *acts], [], [], [], []
    if rows:
        args += [x for part in weights for three in part for x in three]
    if makes:
        args += [tokens, cot]
    if rows:
        args += before
    specs = [SMEM_SPEC] + [VMEM_SPEC] * (len(args) - 1)
    aliases = {}
    if rows:
        if last_rows:
            shape = (2 * last_rows, features)
            outs += [in_vmem(shape, F32)] + [in_vmem(shape, BF16)] * (total // last_rows - 1)
            scratch += [pltpu.VMEM((total, features), F32)] * 2
        else:
            outs += [in_vmem((total, features), F32)] * 2
        out_specs += [VMEM_SPEC] * len(outs)
    if makes:
        aliases = {len(args) + i: len(outs) + i for i in range(len(grads))}
        args += grads
        specs += [HBM_SPEC] * len(grads)
        outs += [
            pltpu.HBM((features, hidden), BF16),
            pltpu.HBM((features, hidden), BF16),
            pltpu.HBM((hidden, features), BF16),
        ]
        out_specs += [HBM_SPEC] * 3
        tile = max(tile_of(piece[-1]) for part in where for piece in part)
        scratch += [
            pltpu.VMEM((SLOTS, 2, features, tile), BF16),
            pltpu.VMEM((SLOTS, tile, features), BF16),
            pltpu.SemaphoreType.DMA((SLOTS, 3)),
        ]
    work = width * features * (rows + makes)
    out = pl.pallas_call(
        functools.partial(
            backward_kernel, where, rows, of or range(len(where)) if makes else (), not before, not grads,
            total // last_rows - 1 if last_rows else 0,
        ),
        in_specs=specs,
        out_specs=out_specs,
        out_shape=outs,
        scratch_shapes=scratch,
        input_output_aliases=aliases,
        compiler_params=params(),
        cost_estimate=cost(6 * total * work, 6 * work),
        name="output_rows" if not makes else "weight_grads" if not rows else "backward",
    )(*args)
    return (out[:-3], out[-3:]) if makes else (out, None)


def finish_kernel(*refs):
    mine, received, (output, grad_input) = refs[0], refs[1:-2], refs[-2:]
    rows = output.shape[0]
    total = mine[...]
    for r in received:
        total = total + r[...].astype(F32)
    output[...] = total[:rows].astype(BF16)
    grad_input[...] = total[rows:].astype(BF16)


def finish(mine, received):
    shape = jax.ShapeDtypeStruct((mine.shape[0] // 2, mine.shape[1]), BF16)
    return pl.pallas_call(
        finish_kernel,
        in_specs=[VMEM_SPEC] * (1 + len(received)),
        out_specs=[VMEM_SPEC] * 2,
        out_shape=[shape] * 2,
        compiler_params=params(),
        name="finish_rows",
    )(mine, *received)


def chunk_parts(hidden, inner):
    units = hidden // inner
    if units % 2048 == 0:
        chunks = [[units * share // 16 for share in chunk] for chunk in CHUNKS]
    else:
        chunks = [[units // 2]] * 2 if units % 256 == 0 else [[units]]
    parts, start = [], 0
    for widths in chunks:
        stride = sum(widths)
        parts.append([
            [(start, core, inner, stride, sum(widths[:i]), w) for i, w in enumerate(widths)]
            for core in range(inner)
        ])
        start += inner * stride
    return parts


def tied(acts, held):
    acts, arrays = lax.optimization_barrier((acts, list(held.values())))
    return acts, dict(zip(held, arrays))


def body(sizes, tokens, cotangent, w_gate, w_up, w_down):
    wide, narrow, inner = sizes["wide"], sizes["narrow"], sizes["inner"]
    rows = tokens.shape[0]
    hidden = w_gate.shape[1]
    me = lax.axis_index("inner").astype(jnp.int32).reshape(1)
    parts = chunk_parts(hidden, inner)
    whole = tuple(in_hbm(w) for w in (w_gate, w_up, w_down))

    packed = pack(tokens, cotangent)
    acts = [packed] + [shift(packed, "wide", wide, k) for k in range(1, wide)]
    uses = [pieces for mine, other in parts for pieces in (other, mine)]
    queue = [piece for pieces in uses for piece in pieces]
    plan, seen = [[]], 0
    while queue and (not plan[0] or 2 * (seen + queue[0][-1]) <= hidden):
        seen += queue[0][-1]
        plan[0].append(queue.pop(0))
    for i in range(len(uses)):
        plan.append([queue.pop(0)] if queue else [])
        while queue and i + 1 < len(uses) and queue[0] in uses[i + 1]:
            plan[-1].append(queue.pop(0))
    held = dict(zip(plan[0], load(me, plan[0], whole)))
    acts, held = tied(acts, held)
    kept, products, crossed, steps = [], [], [], []
    step = 1
    for mine, other in parts:
        made = []
        for pieces, dtype in ((other, BF16), (mine, F32)):
            weights = [held[piece] for piece in pieces]
            out, acts, loaded = forward(
                me, pieces, acts, weights, rows, dtype, plan[step], whole
            )
            held.update(zip(plan[step], loaded))
            step += 1
            made.append(out)
        products.append(made)
        if mine is parts[0][0]:
            spans = [([m], [o]) for m, o in zip(mine, other)]
        else:
            spans = [(mine, other)]
        widths = [sum(p[-1] for p in span[0]) for span in spans]
        joined = join(made[1], shift(made[0], "inner", inner, 1), widths)
        acts, _ = lax.optimization_barrier((acts, joined[-1][1]))
        for span, (total, out) in zip(spans, joined):
            steps.append(span)
            kept.append(total)
            crossed.append([shift(out, "narrow", narrow, k) for k in range(1, narrow)])
    tokens_all, cot_all = acts
    crossed[0], _ = lax.optimization_barrier((crossed[0], products[-1]))
    sums, grads, later = (), (), []
    for i, where in enumerate(steps):
        own = activate(kept[i], crossed[i])
        acts = [own, shift(own, "inner", inner, 1)]
        weights = [[held[piece] for piece in pieces] for pieces in where]
        if i == len(steps) - 1:
            later += list(zip(where, acts))
        else:
            sums, grads = backward(
                me, where, acts, weights, tokens_all, cot_all, sums, grads, hidden
            )
            crossed[i + 1], sums = lax.optimization_barrier((crossed[i + 1], sums))
    for last, (pieces, act, three) in enumerate(zip(where, acts, weights)):
        sums, _ = backward(
            me, [pieces], [act], [three], tokens_all, cot_all, sums, None, hidden,
            rows if last else 0,
        )
    back = [shift(sums[k], "wide", wide, -k) for k in range(1, wide)]
    where, acts = zip(*later)
    _, grads = backward(me, where, acts, None, tokens_all, cot_all, None, grads, hidden)
    output, grad_input = finish(sums[0], back)
    return (output, grad_input, *grads)


def solution(mesh):
    rows = P(("groups", "wide"), ("narrow", "inner"))
    return jax.shard_map(
        functools.partial(body, dict(mesh.shape)),
        mesh=mesh,
        in_specs=(
            rows,
            rows,
            P(("narrow", "inner"), "wide"),
            P(("narrow", "inner"), "wide"),
            P("wide", ("narrow", "inner")),
        ),
        out_specs=(
            rows,
            rows,
            P(("groups", "narrow", "inner"), "wide"),
            P(("groups", "narrow", "inner"), "wide"),
            P(("groups", "wide"), ("narrow", "inner")),
        ),
        check_vma=False,
    )
```

```python
import functools

import jax
import jax.numpy as jnp
from jax import lax
from jax.experimental import pallas as pl
from jax.experimental.pallas import tpu as pltpu
from jax.sharding import PartitionSpec as P

F32 = jnp.float32
BF16 = jnp.bfloat16
CHUNKS = ((4, 4), (4, 4))
VMEM_SPEC = pl.BlockSpec(memory_space=pltpu.VMEM)
SMEM_SPEC = pl.BlockSpec(memory_space=pltpu.SMEM)
ANY_SPEC = pl.BlockSpec(memory_space=pl.ANY)
HBM_SPEC = pl.BlockSpec(memory_space=pltpu.MemorySpace.HBM)
LIMIT = 10 << 20
SLOTS = 3


def contract(left, right, left_dim, right_dim):
    return lax.dot_general(
        left, right, (((left_dim,), (right_dim,)), ((), ())), preferred_element_type=F32
    )


def tile_of(width):
    return 256 if width % 256 == 0 else 128


def params(**more):
    return pltpu.CompilerParams(vmem_limit_bytes=LIMIT, **more)


def cost(flops, moved):
    return pl.CostEstimate(flops=int(flops), bytes_accessed=int(moved), transcendentals=0)


def shift(x, axis, size, by):
    return lax.ppermute(x, axis, [(i, (i + by) % size) for i in range(size)])


def column(me_ref, piece):
    start, core, inner, stride, at, _ = piece
    return pl.multiple_of(start + lax.rem(me_ref[0] + core, inner) * stride + at, 128)


def in_vmem(shape, dtype):
    return pltpu.VMEM(shape, dtype)


def in_hbm(x):
    return pltpu.with_memory_space_constraint(x, pltpu.MemorySpace.HBM)


def piece_copies(me, pieces, whole, out, sems):
    copies = []
    for i, piece in enumerate(pieces):
        here = pl.ds(column(me, piece), piece[-1])
        for j in range(3):
            source = whole[j].at[here, :] if j == 2 else whole[j].at[:, here]
            copies.append(pltpu.make_async_copy(source, out[3 * i + j], sems.at[i, j]))
    return copies


def piece_shapes(pieces, features):
    shapes = []
    for piece in pieces:
        shapes += [in_vmem((features, piece[-1]), BF16)] * 2
        shapes += [in_vmem((piece[-1], features), BF16)]
    return shapes


def in_threes(arrays):
    return [tuple(arrays[i : i + 3]) for i in range(0, len(arrays), 3)]


def load_kernel(pieces, me, *refs):
    copies = piece_copies(me, pieces, refs[:3], refs[3:-1], refs[-1])
    for copy in copies:
        copy.start()
    for copy in copies:
        copy.wait()


def load(me, pieces, whole):
    outs = piece_shapes(pieces, whole[0].shape[0])
    moved = 6 * sum(piece[-1] for piece in pieces) * whole[0].shape[0]
    return in_threes(
        pl.pallas_call(
            functools.partial(load_kernel, pieces),
            in_specs=[SMEM_SPEC] + [HBM_SPEC] * 3,
            out_specs=[VMEM_SPEC] * len(outs),
            out_shape=outs,
            scratch_shapes=[pltpu.SemaphoreType.DMA((len(pieces), 3))],
            compiler_params=params(),
            cost_estimate=cost(0, moved),
            name="load_weights",
        )(me, *whole)
    )


def pack_kernel(tokens, cot, packed, sems):
    rows = tokens.shape[0]
    copies = [
        pltpu.make_async_copy(tokens, packed.at[:rows], sems.at[0]),
        pltpu.make_async_copy(cot, packed.at[rows:], sems.at[1]),
    ]
    for copy in copies:
        copy.start()
    for copy in copies:
        copy.wait()


def pack(tokens, cot):
    return pl.pallas_call(
        pack_kernel,
        in_specs=[ANY_SPEC] * 2,
        out_specs=VMEM_SPEC,
        out_shape=in_vmem((2 * tokens.shape[0], tokens.shape[1]), BF16),
        scratch_shapes=[pltpu.SemaphoreType.DMA((2,))],
        compiler_params=params(),
        cost_estimate=cost(0, 8 * tokens.size),
        name="pack_rows",
    )(in_hbm(tokens), in_hbm(cot))


def forward_kernel(rows, pieces, ahead, out_dtype, count, assemble, me, *refs):
    refs = list(refs)
    take = lambda n: [refs.pop(0) for _ in range(n)]
    acts, weights = take(count), in_threes(take(3 * len(pieces)))
    whole = take(3 if ahead else 0)
    (sums,) = take(1)
    tokens_ref, cot_ref = take(2) if assemble else acts
    copies = []
    if ahead:
        out = take(3 * len(ahead))
        copies = piece_copies(me, ahead, whole, out, *take(1))
    for copy in copies:
        copy.start()

    def compute():
        if assemble:
            for k, piece in enumerate(acts):
                tokens_ref[pl.ds(k * rows, rows), :] = piece[:rows, :]
                cot_ref[pl.ds(k * rows, rows), :] = piece[rows:, :]
        tokens, cot = tokens_ref[...], cot_ref[...]
        first = 0
        for (w_gate, w_up, w_down), piece in zip(weights, pieces):
            tile = tile_of(piece[-1])
            for start in range(0, piece[-1], tile):
                here = slice(start, start + tile)
                there = slice(first, first + tile)
                first += tile
                sums[0, :, there] = contract(tokens, w_gate[:, here], 1, 0).astype(out_dtype)
                sums[1, :, there] = contract(tokens, w_up[:, here], 1, 0).astype(out_dtype)
                sums[2, :, there] = contract(cot, w_down[here, :], 1, 1).astype(out_dtype)

    if ahead:
        pl.when(me[0] >= 0)(compute)
    else:
        compute()
    for copy in copies:
        copy.wait()


def forward(me, pieces, acts, weights, rows, out_dtype, ahead, whole):
    assemble = len(acts) != 2
    features = acts[0].shape[1]
    width = sum(piece[-1] for piece in pieces)
    total = rows * len(acts) if assemble else acts[0].shape[0]
    whole = whole if ahead else ()
    outs = [in_vmem((3, total, width), out_dtype)]
    if assemble:
        outs += [in_vmem((total, features), BF16)] * 2
    outs += piece_shapes(ahead, features)
    out = pl.pallas_call(
        functools.partial(
            forward_kernel, rows, pieces, ahead, out_dtype, len(acts), assemble
        ),
        in_specs=[SMEM_SPEC]
        + [VMEM_SPEC] * (len(acts) + 3 * len(pieces))
        + [HBM_SPEC] * len(whole),
        out_specs=[VMEM_SPEC] * len(outs),
        out_shape=outs,
        scratch_shapes=[pltpu.SemaphoreType.DMA((len(ahead), 3))] * bool(ahead),
        compiler_params=params(),
        cost_estimate=cost(6 * total * width, 6 * total * width),
        name="partial_sums",
    )(me, *acts, *(x for three in weights for x in three), *whole)
    loaded = in_threes(out[len(out) - 3 * len(ahead) :]) if ahead else []
    return out[0], out[1:3] if assemble else acts, loaded


def join_kernel(mine, received, *outs):
    first = 0
    for kept, sent in zip(outs[0::2], outs[1::2]):
        here = slice(first, first + kept.shape[2])
        first += kept.shape[2]
        total = mine[:, :, here] + received[:, :, here].astype(F32)
        kept[...] = total
        sent[...] = total.astype(BF16)


def join(mine, received, widths):
    outs = []
    for width in widths:
        outs += [in_vmem((*mine.shape[:2], width), dtype) for dtype in (F32, BF16)]
    out = pl.pallas_call(
        join_kernel,
        in_specs=[VMEM_SPEC] * 2,
        out_specs=[VMEM_SPEC] * len(outs),
        out_shape=outs,
        compiler_params=params(),
        cost_estimate=cost(mine.size, 12 * mine.size),
        name="join_cores",
    )(mine, received)
    return list(zip(out[0::2], out[1::2]))


def activate_kernel(*refs):
    kept, received, out = refs[0], refs[1:-1], refs[-1]
    gate, up, upstream = [
        sum((r[i].astype(F32) for r in received), kept[i]) for i in range(3)
    ]
    sigmoid = 1.0 / (1.0 + jnp.exp(-gate))
    swish = gate * sigmoid
    out[0] = (swish * up).astype(BF16)
    out[1] = (upstream * up * sigmoid * (1.0 + gate * (1.0 - sigmoid))).astype(BF16)
    out[2] = (upstream * swish).astype(BF16)


def activate(kept, received):
    return pl.pallas_call(
        activate_kernel,
        in_specs=[VMEM_SPEC] * (1 + len(received)),
        out_specs=VMEM_SPEC,
        out_shape=in_vmem(kept.shape, BF16),
        compiler_params=params(),
        cost_estimate=cost(8 * kept.size, 8 * kept.size),
        name="activation",
    )(kept, *received)


def backward_kernel(where, rows, grads, first, fresh, last, me, *refs):
    refs = list(refs)
    take = lambda n: [refs.pop(0) for _ in range(n)]
    acts = take(len(where))
    weights = [in_threes(take(3 * len(p))) if rows else [None] * len(p) for p in where]
    tokens, cot = take(2) if grads else (None, None)
    before = take(2) if rows and not first else None
    if grads and not fresh:
        take(3)
    sums = take(1 + last if last else 2) if rows else None
    outs = take(3) if grads else None
    out_acc, grad_acc = (take(2) if last else sums) if rows else (None, None)
    if grads:
        wide, tall, sems = take(3)
    slots = sems.shape[0] if grads else 1

    def copies(slot, at, tile):
        here = pl.ds(at, tile)
        cols = pl.ds(0, tile)
        return [
            pltpu.make_async_copy(
                wide.at[slot, 0, :, cols], outs[0].at[:, here], sems.at[slot, 0]
            ),
            pltpu.make_async_copy(
                wide.at[slot, 1, :, cols], outs[1].at[:, here], sems.at[slot, 1]
            ),
            pltpu.make_async_copy(tall.at[slot, cols], outs[2].at[here, :], sems.at[slot, 2]),
        ]

    if rows:
        if first:
            out_acc[...] = jnp.zeros_like(out_acc)
            grad_acc[...] = jnp.zeros_like(grad_acc)
        else:
            out_acc[...] = before[0][...]
            grad_acc[...] = before[1][...]
    flying, tiles = [], []
    for p, pieces in enumerate(where):
        done = 0
        for three, piece in zip(weights[p], pieces):
            tile = tile_of(piece[-1]) if grads else piece[-1]
            for at in range(0, piece[-1], tile):
                tiles.append((p, slice(done + at, done + at + tile), three, piece, at))
            done += piece[-1]

    def make_grads(p, units, _, piece, at):
        hidden, grad_gate, grad_up = [acts[p][i, :, units] for i in range(3)]
        slot, tile = len(flying) % slots, units.stop - units.start
        if len(flying) >= slots:
            for copy in flying[len(flying) - slots]:
                copy.wait()
        cols = slice(0, tile)
        wide[slot, 0, :, cols] = contract(tokens[...], grad_gate, 0, 0).astype(BF16)
        wide[slot, 1, :, cols] = contract(tokens[...], grad_up, 0, 0).astype(BF16)
        tall[slot, cols] = contract(hidden, cot[...], 0, 0).astype(BF16)
        flying.append(copies(slot, pl.multiple_of(column(me, piece) + at, 128), tile))
        for copy in flying[-1]:
            copy.start()

    def add_rows(p, units, three, piece, at):
        hidden, grad_gate, grad_up = [acts[p][i, :, units] for i in range(3)]
        w_gate, w_up, w_down = three
        here = slice(at, at + units.stop - units.start)
        out_acc[...] += contract(hidden, w_down[here, :], 1, 0)
        grad_acc[...] += contract(grad_gate, w_gate[:, here], 1, 1) + contract(
            grad_up, w_up[:, here], 1, 1
        )

    behind = 2 if grads else 0
    for i in range(len(tiles) + behind):
        if grads and i < len(tiles) and tiles[i][0] in grads:
            make_grads(*tiles[i])
        if rows and i >= behind:
            add_rows(*tiles[i - behind])
    if last:
        n = sums[0].shape[0] // 2
        for k, ref in enumerate(sums):
            ref[:n, :] = out_acc[k * n : (k + 1) * n, :].astype(ref.dtype)
            ref[n:, :] = grad_acc[k * n : (k + 1) * n, :].astype(ref.dtype)
    for group in flying[-slots:]:
        for copy in group:
            copy.wait()


def backward(
    me, where, acts, weights, tokens, cot, before, grads, hidden, last_rows=0, of=None
):
    total = acts[0].shape[1]
    features = tokens.shape[1]
    width = sum(a.shape[2] for a in acts)
    rows, makes = before is not None, grads is not None
    args, specs, outs, out_specs, scratch = [me, *acts], [], [], [], []
    if rows:
        args += [x for part in weights for three in part for x in three]
    if makes:
        args += [tokens, cot]
    if rows:
        args += before
    specs = [SMEM_SPEC] + [VMEM_SPEC] * (len(args) - 1)
    aliases = {}
    if rows:
        if last_rows:
            shape = (2 * last_rows, features)
            outs += [in_vmem(shape, F32)] + [in_vmem(shape, BF16)] * (total // last_rows - 1)
            scratch += [pltpu.VMEM((total, features), F32)] * 2
        else:
            outs += [in_vmem((total, features), F32)] * 2
        out_specs += [VMEM_SPEC] * len(outs)
    if makes:
        aliases = {len(args) + i: len(outs) + i for i in range(len(grads))}
        args += grads
        specs += [HBM_SPEC] * len(grads)
        outs += [
            pltpu.HBM((features, hidden), BF16),
            pltpu.HBM((features, hidden), BF16),
            pltpu.HBM((hidden, features), BF16),
        ]
        out_specs += [HBM_SPEC] * 3
        tile = max(tile_of(piece[-1]) for part in where for piece in part)
        scratch += [
            pltpu.VMEM((SLOTS, 2, features, tile), BF16),
            pltpu.VMEM((SLOTS, tile, features), BF16),
            pltpu.SemaphoreType.DMA((SLOTS, 3)),
        ]
    work = width * features * (rows + makes)
    out = pl.pallas_call(
        functools.partial(
            backward_kernel, where, rows, of or range(len(where)) if makes else (), not before, not grads,
            total // last_rows - 1 if last_rows else 0,
        ),
        in_specs=specs,
        out_specs=out_specs,
        out_shape=outs,
        scratch_shapes=scratch,
        input_output_aliases=aliases,
        compiler_params=params(),
        cost_estimate=cost(6 * total * work, 6 * work),
        name="output_rows" if not makes else "weight_grads" if not rows else "backward",
    )(*args)
    return (out[:-3], out[-3:]) if makes else (out, None)


def finish_kernel(*refs):
    mine, received, (output, grad_input) = refs[0], refs[1:-2], refs[-2:]
    rows = output.shape[0]
    total = mine[...]
    for r in received:
        total = total + r[...].astype(F32)
    output[...] = total[:rows].astype(BF16)
    grad_input[...] = total[rows:].astype(BF16)


def finish(mine, received):
    shape = jax.ShapeDtypeStruct((mine.shape[0] // 2, mine.shape[1]), BF16)
    return pl.pallas_call(
        finish_kernel,
        in_specs=[VMEM_SPEC] * (1 + len(received)),
        out_specs=[VMEM_SPEC] * 2,
        out_shape=[shape] * 2,
        compiler_params=params(),
        name="finish_rows",
    )(mine, *received)


def chunk_parts(hidden, inner):
    units = hidden // inner
    if units % 2048 == 0:
        chunks = [[units * share // 16 for share in chunk] for chunk in CHUNKS]
    else:
        chunks = [[units // 2]] * 2 if units % 256 == 0 else [[units]]
    parts, start = [], 0
    for widths in chunks:
        stride = sum(widths)
        parts.append([
            [(start, core, inner, stride, sum(widths[:i]), w) for i, w in enumerate(widths)]
            for core in range(inner)
        ])
        start += inner * stride
    return parts


def tied(acts, held):
    acts, arrays = lax.optimization_barrier((acts, list(held.values())))
    return acts, dict(zip(held, arrays))


def body(sizes, tokens, cotangent, w_gate, w_up, w_down):
    wide, narrow, inner = sizes["wide"], sizes["narrow"], sizes["inner"]
    rows = tokens.shape[0]
    hidden = w_gate.shape[1]
    me = lax.axis_index("inner").astype(jnp.int32).reshape(1)
    parts = chunk_parts(hidden, inner)
    whole = tuple(in_hbm(w) for w in (w_gate, w_up, w_down))

    packed = pack(tokens, cotangent)
    acts = [packed] + [shift(packed, "wide", wide, k) for k in range(1, wide)]
    uses = [pieces for mine, other in parts for pieces in (other, mine)]
    queue = [piece for pieces in uses for piece in pieces]
    plan, seen = [[]], 0
    while queue and (not plan[0] or 2 * (seen + queue[0][-1]) <= hidden):
        seen += queue[0][-1]
        plan[0].append(queue.pop(0))
    for i in range(len(uses)):
        plan.append([queue.pop(0)] if queue else [])
        while queue and i + 1 < len(uses) and queue[0] in uses[i + 1]:
            plan[-1].append(queue.pop(0))
    held = dict(zip(plan[0], load(me, plan[0], whole)))
    acts, held = tied(acts, held)
    kept, products, crossed, steps = [], [], [], []
    step = 1
    for mine, other in parts:
        made = []
        for pieces, dtype in ((other, BF16), (mine, F32)):
            weights = [held[piece] for piece in pieces]
            out, acts, loaded = forward(
                me, pieces, acts, weights, rows, dtype, plan[step], whole
            )
            held.update(zip(plan[step], loaded))
            step += 1
            made.append(out)
        products.append(made)
        if mine is parts[0][0]:
            spans = [([m], [o]) for m, o in zip(mine, other)]
        else:
            spans = [(mine, other)]
        widths = [sum(p[-1] for p in span[0]) for span in spans]
        joined = join(made[1], shift(made[0], "inner", inner, 1), widths)
        acts, _ = lax.optimization_barrier((acts, joined[-1][1]))
        for span, (total, out) in zip(spans, joined):
            steps.append(span)
            kept.append(total)
            crossed.append([shift(out, "narrow", narrow, k) for k in range(1, narrow)])
    tokens_all, cot_all = acts
    crossed[0], _ = lax.optimization_barrier((crossed[0], products[-1]))
    sums, grads, later = (), (), []
    for i, where in enumerate(steps):
        own = activate(kept[i], crossed[i])
        acts = [own, shift(own, "inner", inner, 1)]
        weights = [[held[piece] for piece in pieces] for pieces in where]
        if i == len(steps) - 1:
            later += list(zip(where, acts))
        else:
            sums, grads = backward(
                me, where, acts, weights, tokens_all, cot_all, sums, grads, hidden
            )
            crossed[i + 1], sums = lax.optimization_barrier((crossed[i + 1], sums))
    for last, (pieces, act, three) in enumerate(zip(where, acts, weights)):
        sums, _ = backward(
            me, [pieces], [act], [three], tokens_all, cot_all, sums, None, hidden,
            rows if last else 0,
        )
    back = [shift(sums[k], "wide", wide, -k) for k in range(1, wide)]
    where, acts = zip(*later)
    _, grads = backward(me, where, acts, None, tokens_all, cot_all, None, grads, hidden)
    output, grad_input = finish(sums[0], back)
    return (output, grad_input, *grads)


def solution(mesh):
    rows = P(("groups", "wide"), ("narrow", "inner"))
    return jax.shard_map(
        functools.partial(body, dict(mesh.shape)),
        mesh=mesh,
        in_specs=(
            rows,
            rows,
            P(("narrow", "inner"), "wide"),
            P(("narrow", "inner"), "wide"),
            P("wide", ("narrow", "inner")),
        ),
        out_specs=(
            rows,
            rows,
            P(("groups", "narrow", "inner"), "wide"),
            P(("groups", "narrow", "inner"), "wide"),
            P(("groups", "wide"), ("narrow", "inner")),
        ),
        check_vma=False,
    )
```
